32 devices in a mesh: line: 8 (over z, core), bus: 4 (over y, x).
Axes of the slice: x: 2, y: 2, z: 4, core: 2. Of those that a mesh axis runs over, the one named last changes fastest.
Arguments:
- ptdf: bfloat16 [8192, 70656], P('line', 'bus'), may hold values from -0.0234375 to 0.0234375
- injections: bfloat16 [70656, 256], P('bus', 'line'), may hold values from -6 to 6
- viol_mask: int32 [8192, 256], P('line'), may hold values 0 or 1
- viol_sign: int32 [8192], P('line'), may hold values from 0 to 1
- limit: float32 [8192], P('line'), may hold values from 0.2 to 1.5
- price: float32 [8192], P('line'), may hold values from 0.3 to 3
- owner: int32 [70656], P('bus'), may hold values from 0 to 10367, as said below
Outputs:
- gen_cut: float32 [10368, 256], P(('line', 'bus'))
The draws below stay inside these ranges and needn't reach their ends.
Inputs may be any that keep to these rules, and one draw needn't show every extreme that they name: `owner`: each bus has one owning generator; split the buses into aligned blocks of 70656 // 32 in order and the generators into groups of 10368 // 32 in order: in every block at most 69 buses belong to one group, and some group has exactly 69 in every block.
All inputs are finite; a program needn't handle non-finite values. No bound on the sum of `viol_mask` on one device may be relied on, other than what follows from the above.
Results may differ from the reference program's by a relative error of at most 0.0029.
Values may be sent and summed in bfloat16 or wider, within the bound.
A program may use at most 128 MiB of HBM per device.

```python
import math
import jax
import jax.numpy as jnp
from jax import lax

LINE_DEV = 1024
BUSES = 70656
SCEN = 256
GENS = 10368
LINES = 8192
DEVICES = 32


def draw_owner(key, part):
    devices = DEVICES
    block_rows = BUSES // devices
    held_gens = GENS // devices
    first, second, third = jax.random.split(key, 3)
    order = jax.vmap(lambda k: jax.random.permutation(k, block_rows))(jax.random.split(first, devices))
    target_perm = jax.vmap(lambda k: jax.random.permutation(k, devices))(jax.random.split(second, devices))
    target = jnp.take_along_axis(target_perm, order % devices, axis=1)
    within = jax.random.randint(third, (devices, block_rows), 0, held_gens)
    return (target * held_gens + within).reshape(BUSES).astype(jnp.int32)


def set_ends(array, key, low, high):
    extent = array.shape
    spot = [jax.random.randint(jax.random.fold_in(key, axis), (), 0, extent[axis]) for axis in range(len(extent))]
    array = array.at[tuple(spot)].set(low)
    longest = extent.index(max(extent))
    spot[longest] = (spot[longest] + 1) % extent[longest]
    return array.at[tuple(spot)].set(high)


def block_levels(rng, shape, shards, least, high):
    factor_of = 1.0
    for axis_at, blocks in shards:
        steps = jax.random.uniform(jax.random.fold_in(jax.random.fold_in(rng, 6), axis_at), (blocks,), jnp.float32, least / len(shards), high / len(shards))
        factor_of = factor_of * jnp.repeat(jnp.exp(steps), shape[axis_at] // blocks).reshape((-1,) + (1,) * (len(shape) - 1 - axis_at))
    return factor_of


def normal_values(key, shape, width, bound, cuts=(), dtype=jnp.bfloat16):
    array = width * jax.random.normal(key, shape, jnp.float32)
    if cuts:
        array = array * block_levels(key, shape, cuts, -0.22, 0.18)
    return jnp.clip(array, -bound, bound).astype(dtype)


def setup_inputs(seed: int = 0) -> dict:
    streams_of = jax.random.split(jax.random.key(seed), 8)
    return {
        "ptdf": normal_values(streams_of[0], (LINES, BUSES), BUSES ** -0.5, 0.0234375, ((0, 8), (1, 4))),
        "injections": normal_values(streams_of[1], (BUSES, SCEN), 1.0, 6.0, ((0, 4), (1, 8))),
        "viol_mask": set_ends((jax.random.randint(streams_of[2], (LINES, SCEN), 0, 3) < 1).astype(jnp.int32), jax.random.fold_in(streams_of[2], 1), 0, 1),
        "viol_sign": set_ends(jax.random.randint(streams_of[3], (LINES,), 0, 2), jax.random.fold_in(streams_of[3], 1), 0, 1).astype(jnp.int32),
        "limit": jnp.clip(0.2 + 1.3 * jax.random.uniform(streams_of[4], (LINES,), jnp.float32) ** block_levels(streams_of[4], (LINES,), ((0, 8),), -0.2, 0.2), 0.2, 1.5),
        "price": jnp.clip(jnp.exp(math.log(3.0) - 2.3025851 * jax.random.uniform(streams_of[5], (LINES,), jnp.float32) ** block_levels(streams_of[5], (LINES,), ((0, 8),), -0.2, 0.2)), 0.3, 3.0),
        "owner": draw_owner(jax.random.fold_in(streams_of[7], 71), 0),
    }


def reference(ptdf, injections, viol_mask, viol_sign, limit, price, owner):
    blocks = LINES // LINE_DEV
    slab = ptdf.reshape(blocks, LINE_DEV, BUSES)
    masks = viol_mask.reshape(blocks, LINE_DEV, SCEN)
    signs = viol_sign.reshape(blocks, LINE_DEV)
    limits = limit.reshape(blocks, LINE_DEV)
    prices = price.reshape(blocks, LINE_DEV)
    inject32 = injections.astype(jnp.float32)

    def step(total, items):
        rows, mrows, srows, lrows, prows = items
        rows32 = rows.astype(jnp.float32)
        flows = jnp.dot(rows32, inject32, precision=lax.Precision.HIGHEST)
        direction = (2 * srows - 1).astype(jnp.float32)[:, None]
        dual = (mrows.astype(jnp.float32) * prows[:, None] * (direction * flows - lrows[:, None])).astype(jnp.bfloat16)
        total = total + jnp.dot(rows32.T, dual.astype(jnp.float32), precision=lax.Precision.HIGHEST)
        return total, None

    start = jnp.zeros((BUSES, SCEN), jnp.float32)
    cuts, unused = lax.scan(step, start, (slab, masks, signs, limits, prices))
    return jax.ops.segment_sum(cuts, owner, num_segments=GENS)
```

```python
import functools
import jax
import jax.numpy as jnp
from jax import lax
from jax.experimental import pallas as pl
from jax.experimental.pallas import tpu as pltpu
from jax.sharding import PartitionSpec as P

BUSES = 70656
GENS = 10368
LANES = 128
GROUPS_STEP = 8
GATHER_CHUNKS = 2
SUM_CHUNKS = 2


def round_up(value, unit):
    return (value + unit - 1) // unit * unit


def make_dual(flows, mask_part, viol_sign, limit, price):
    direction = (2 * viol_sign - 1).astype(jnp.float32)[:, None]
    return (
        mask_part.astype(jnp.float32) * price[:, None] * (direction * flows - limit[:, None])
    ).astype(jnp.bfloat16)


def place_buses(owner, n_line, n_bus):
    devices = n_line * n_bus
    block_rows = BUSES // devices
    held = GENS // devices
    blocks = owner.shape[0] // block_rows
    slots = round_up((block_rows + devices - 1) // devices, 16)
    owner = owner.reshape(blocks, block_rows)
    target = owner // held
    per = n_line // SUM_CHUNKS
    line_of, bus_of = target // n_bus, target % n_bus
    group = (line_of // per) * (n_bus * per) + bus_of * per + line_of % per
    hits = group[:, None, :] == jnp.arange(devices, dtype=jnp.int32)[None, :, None]
    before = jnp.arange(block_rows)[:, None] < jnp.arange(block_rows)[None, :]
    earlier = jnp.einsum(
        "bgk,kj->bgj",
        hits.astype(jnp.bfloat16),
        before.astype(jnp.bfloat16),
        preferred_element_type=jnp.float32,
    )
    place = jnp.sum(jnp.where(hits, earlier, 0.0), axis=1).astype(jnp.int32)
    base = jnp.arange(blocks, dtype=jnp.int32)[:, None] * (devices * slots)
    slot = (base + group * slots + place).reshape(1, blocks * block_rows)
    at_place = place[:, None, :] == jnp.arange(slots, dtype=jnp.int32)[None, :, None]
    held_id = jnp.where(hits, (owner % held)[:, None, :], 0).astype(jnp.float32)
    slot_gen = jnp.einsum(
        "bgk,bpk->gbp", held_id, at_place.astype(jnp.float32), precision=lax.Precision.HIGHEST
    )
    slot_gen = jnp.round(slot_gen).astype(jnp.int32).reshape(devices, 1, blocks * slots)
    return slot, slot_gen, slots, blocks


def sum_kernel(slots, blocks, block_rows, window, first_group, devices_slots, cuts_ref, slot_ref, gen_ref, out_ref, picked):
    rows = GROUPS_STEP * slots
    total = cuts_ref.shape[1]
    first = pl.program_id(0) * rows + first_group * slots

    def pick(block, carry):
        start = jnp.minimum(block * block_rows // LANES * LANES, total - window)
        span = pl.ds(pl.multiple_of(start, LANES), window)
        ids = lax.broadcasted_iota(jnp.int32, (rows, window), 0)
        wanted = slot_ref[:, span] - (first + block * devices_slots)
        choose = (ids == wanted).astype(jnp.bfloat16)
        got = lax.dot_general(
            choose, cuts_ref[:, span], (((1,), (1,)), ((), ())), preferred_element_type=jnp.float32
        )
        for item in range(GROUPS_STEP):
            picked[item, pl.ds(pl.multiple_of(block * slots, 16), slots), :] = got[
                item * slots : (item + 1) * slots
            ].astype(jnp.bfloat16)
        return carry

    lax.fori_loop(0, blocks, pick, 0)
    held = out_ref.shape[1]
    ids = lax.broadcasted_iota(jnp.int32, (held, blocks * slots), 0)
    for item in range(GROUPS_STEP):
        choose = (ids == gen_ref[item]).astype(jnp.bfloat16)
        out_ref[item] = jnp.dot(
            choose, picked[item], preferred_element_type=jnp.float32
        ).astype(out_ref.dtype)


def sum_owned(cuts_t, slot, slot_gen, slots, blocks, held_pad, first_group, groups):
    scen, total = cuts_t.shape
    devices = slot_gen.shape[0]
    block_rows = total // blocks
    reach = max((b * block_rows) % LANES for b in range(blocks)) + block_rows
    window = min(round_up(reach, LANES), total)
    step0 = first_group // GROUPS_STEP
    return pl.pallas_call(
        functools.partial(
            sum_kernel, slots, blocks, block_rows, window, first_group, devices * slots
        ),
        grid=(groups // GROUPS_STEP,),
        out_shape=jax.ShapeDtypeStruct((groups, held_pad, scen), jnp.float32),
        in_specs=[
            pl.BlockSpec((scen, total), lambda i: (0, 0)),
            pl.BlockSpec((1, total), lambda i: (0, 0)),
            pl.BlockSpec((GROUPS_STEP, 1, blocks * slots), lambda i: (i + step0, 0, 0)),
        ],
        out_specs=pl.BlockSpec((GROUPS_STEP, held_pad, scen), lambda i: (i, 0, 0)),
        scratch_shapes=[pltpu.VMEM((GROUPS_STEP, blocks * slots, scen), jnp.bfloat16)],
        compiler_params=pltpu.CompilerParams(vmem_limit_bytes=48 * 1024 * 1024),
        cost_estimate=pl.CostEstimate(
            flops=2 * groups * blocks * slots * (window + held_pad) * scen,
            bytes_accessed=2 * scen * total + 4 * groups * held_pad * scen,
            transcendentals=0,
        ),
        name="sum_owned",
    )(cuts_t, slot, slot_gen)


def local(ptdf, injections, viol_mask, viol_sign, limit, price, owner):
    n_line, n_bus = lax.axis_size("line"), lax.axis_size("bus")
    devices = n_line * n_bus
    held = GENS // devices
    held_pad = round_up(held, 8)
    slot, slot_gen, slots, blocks = place_buses(owner, n_line, n_bus)

    width = injections.shape[0] // GATHER_CHUNKS
    partial_flows = None
    for part in range(GATHER_CHUNKS):
        span = slice(part * width, (part + 1) * width)
        gathered = lax.all_gather(injections[span], "line", axis=1, tiled=True)
        if part == GATHER_CHUNKS - 1:
            gathered, slot, slot_gen = lax.optimization_barrier((gathered, slot, slot_gen))
        term = jnp.dot(ptdf[:, span], gathered, preferred_element_type=jnp.float32)
        partial_flows = term if partial_flows is None else partial_flows + term

    flows = lax.psum_scatter(partial_flows, "bus", scatter_dimension=0, tiled=True)
    lines = flows.shape[0]
    mine = lax.axis_index("bus") * lines
    own = lambda a: lax.dynamic_slice_in_dim(a, mine, lines, 0)
    dual = make_dual(flows, own(viol_mask), own(viol_sign), own(limit), own(price))
    dual = lax.all_gather(dual, "bus", axis=0, tiled=True)

    cuts_t = lax.dot_general(
        dual, ptdf, (((0,), (0,)), ((), ())), preferred_element_type=jnp.float32
    ).astype(jnp.bfloat16)
    groups = devices // SUM_CHUNKS
    pieces = []
    for part in range(SUM_CHUNKS):
        sums = sum_owned(
            cuts_t, slot, slot_gen, slots, blocks, held_pad, part * groups, groups
        )
        sums = sums.reshape(n_bus, n_line // SUM_CHUNKS, held_pad, sums.shape[-1])
        pieces.append(lax.psum_scatter(sums, "bus", scatter_dimension=0, tiled=True)[0])
    sums = jnp.concatenate(pieces, axis=0)
    sums = lax.psum_scatter(sums, "line", scatter_dimension=0, tiled=True)[0]
    return sums[:held]


def solution(mesh):
    placed = (
        P("line", "bus"),
        P("bus", "line"),
        P("line", None),
        P("line"),
        P("line"),
        P("line"),
        P("bus"),
    )
    return jax.shard_map(
        local, mesh=mesh, in_specs=placed, out_specs=P(("line", "bus"), None), check_vma=False
    )
```

```python
import functools
import jax
import jax.numpy as jnp
from jax import lax
from jax.experimental import pallas as pl
from jax.experimental.pallas import tpu as pltpu
from jax.sharding import PartitionSpec as P

BUSES = 70656
GENS = 10368
LANES = 128
GROUPS_STEP = 8
SUM_CHUNKS = 2


def round_up(value, unit):
    return (value + unit - 1) // unit * unit


def make_dual(flows, mask_part, viol_sign, limit, price):
    direction = (2 * viol_sign - 1).astype(jnp.float32)[:, None]
    return (
        mask_part.astype(jnp.float32) * price[:, None] * (direction * flows - limit[:, None])
    ).astype(jnp.bfloat16)


def place_buses(owner, n_line, n_bus):
    devices = n_line * n_bus
    block_rows = BUSES // devices
    held = GENS // devices
    blocks = owner.shape[0] // block_rows
    slots = round_up((block_rows + devices - 1) // devices, 16)
    owner = owner.reshape(blocks, block_rows)
    target = owner // held
    per = n_line // SUM_CHUNKS
    line_of, bus_of = target // n_bus, target % n_bus
    group = (line_of // per) * (n_bus * per) + bus_of * per + line_of % per
    hits = group[:, None, :] == jnp.arange(devices, dtype=jnp.int32)[None, :, None]
    before = jnp.arange(block_rows)[:, None] < jnp.arange(block_rows)[None, :]
    earlier = jnp.einsum(
        "bgk,kj->bgj",
        hits.astype(jnp.bfloat16),
        before.astype(jnp.bfloat16),
        preferred_element_type=jnp.float32,
    )
    place = jnp.sum(jnp.where(hits, earlier, 0.0), axis=1).astype(jnp.int32)
    base = jnp.arange(blocks, dtype=jnp.int32)[:, None] * (devices * slots)
    slot = (base + group * slots + place).reshape(1, blocks * block_rows)
    at_place = place[:, None, :] == jnp.arange(slots, dtype=jnp.int32)[None, :, None]
    held_id = jnp.where(hits, (owner % held)[:, None, :], 0).astype(jnp.float32)
    slot_gen = jnp.einsum(
        "bgk,bpk->gbp", held_id, at_place.astype(jnp.float32), precision=lax.Precision.HIGHEST
    )
    slot_gen = jnp.round(slot_gen).astype(jnp.int32).reshape(devices, 1, blocks * slots)
    return slot, slot_gen, slots, blocks


def sum_kernel(slots, blocks, block_rows, window, first_group, devices_slots, cuts_ref, slot_ref, gen_ref, out_ref, picked):
    rows = GROUPS_STEP * slots
    total = cuts_ref.shape[1]
    first = pl.program_id(0) * rows + first_group * slots

    def pick(block, carry):
        start = jnp.minimum(block * block_rows // LANES * LANES, total - window)
        span = pl.ds(pl.multiple_of(start, LANES), window)
        ids = lax.broadcasted_iota(jnp.int32, (rows, window), 0)
        wanted = slot_ref[:, span] - (first + block * devices_slots)
        choose = (ids == wanted).astype(jnp.bfloat16)
        got = lax.dot_general(
            choose, cuts_ref[:, span], (((1,), (1,)), ((), ())), preferred_element_type=jnp.float32
        )
        for item in range(GROUPS_STEP):
            picked[item, pl.ds(pl.multiple_of(block * slots, 16), slots), :] = got[
                item * slots : (item + 1) * slots
            ].astype(jnp.bfloat16)
        return carry

    lax.fori_loop(0, blocks, pick, 0)
    held = out_ref.shape[1]
    ids = lax.broadcasted_iota(jnp.int32, (held, blocks * slots), 0)
    for item in range(GROUPS_STEP):
        choose = (ids == gen_ref[item]).astype(jnp.bfloat16)
        out_ref[item] = jnp.dot(
            choose, picked[item], preferred_element_type=jnp.float32
        ).astype(out_ref.dtype)


def sum_owned(cuts_t, slot, slot_gen, slots, blocks, held_pad, first_group, groups):
    scen, total = cuts_t.shape
    devices = slot_gen.shape[0]
    block_rows = total // blocks
    reach = max((b * block_rows) % LANES for b in range(blocks)) + block_rows
    window = min(round_up(reach, LANES), total)
    step0 = first_group // GROUPS_STEP
    return pl.pallas_call(
        functools.partial(
            sum_kernel, slots, blocks, block_rows, window, first_group, devices * slots
        ),
        grid=(groups // GROUPS_STEP,),
        out_shape=jax.ShapeDtypeStruct((groups, held_pad, scen), jnp.float32),
        in_specs=[
            pl.BlockSpec((scen, total), lambda i: (0, 0)),
            pl.BlockSpec((1, total), lambda i: (0, 0)),
            pl.BlockSpec((GROUPS_STEP, 1, blocks * slots), lambda i: (i + step0, 0, 0)),
        ],
        out_specs=pl.BlockSpec((GROUPS_STEP, held_pad, scen), lambda i: (i, 0, 0)),
        scratch_shapes=[pltpu.VMEM((GROUPS_STEP, blocks * slots, scen), jnp.bfloat16)],
        compiler_params=pltpu.CompilerParams(vmem_limit_bytes=48 * 1024 * 1024),
        cost_estimate=pl.CostEstimate(
            flops=2 * groups * blocks * slots * (window + held_pad) * scen,
            bytes_accessed=2 * scen * total + 4 * groups * held_pad * scen,
            transcendentals=0,
        ),
        name="sum_owned",
    )(cuts_t, slot, slot_gen)


def halve_over_bus(sums, masks, wire):
    n_bus = sums.shape[0]
    bits = n_bus.bit_length() - 1
    me = lax.axis_index("bus")
    rest = sums.shape[1:]
    sums = sums.reshape((2,) * bits + rest)
    open_masks = [1 << (bits - 1 - axis) for axis in range(bits)]
    for mask in masks:
        axis = open_masks.index(mask)
        open_masks.pop(axis)
        side = (me // mask) % 2
        kept = lax.dynamic_index_in_dim(sums, side, axis, keepdims=False)
        sent = lax.dynamic_index_in_dim(sums, 1 - side, axis, keepdims=False)
        pairs = [(i, i ^ mask) for i in range(n_bus)]
        got = lax.ppermute(sent.astype(wire), "bus", pairs)
        sums = kept + got.astype(jnp.float32)
    return sums


def local(ptdf, injections, viol_mask, viol_sign, limit, price, owner):
    n_line, n_bus = lax.axis_size("line"), lax.axis_size("bus")
    devices = n_line * n_bus
    held = GENS // devices
    held_pad = round_up(held, 8)
    slot, slot_gen, slots, blocks = place_buses(owner, n_line, n_bus)

    buses = injections.shape[0]
    cut = buses // 2 // LANES * LANES
    partial_flows = None
    for span in (slice(0, cut), slice(cut, buses)):
        gathered = lax.all_gather(injections[span], "line", axis=1, tiled=True)
        if span.stop == buses:
            gathered, slot, slot_gen = lax.optimization_barrier((gathered, slot, slot_gen))
        term = jnp.dot(ptdf[:, span], gathered, preferred_element_type=jnp.float32)
        partial_flows = term if partial_flows is None else partial_flows + term

    masks = [1 << bit for bit in range(n_bus.bit_length() - 1)]
    lines, scen = partial_flows.shape[0] // n_bus, partial_flows.shape[1]
    halves = partial_flows.reshape(n_bus, lines, scen)
    flows = jnp.concatenate(
        [
            halve_over_bus(halves[..., : scen // 2], masks, jnp.float32),
            halve_over_bus(halves[..., scen // 2 :], masks[::-1], jnp.float32),
        ],
        axis=1,
    )
    mine = lax.axis_index("bus") * lines
    own = lambda a: lax.dynamic_slice_in_dim(a, mine, lines, 0)
    dual = make_dual(flows, own(viol_mask), own(viol_sign), own(limit), own(price))
    dual = lax.all_gather(dual, "bus", axis=0, tiled=True)

    cuts_t = lax.dot_general(
        dual, ptdf, (((0,), (0,)), ((), ())), preferred_element_type=jnp.float32
    ).astype(jnp.bfloat16)
    groups = devices // SUM_CHUNKS
    pieces = []
    for part in range(SUM_CHUNKS):
        sums = sum_owned(
            cuts_t, slot, slot_gen, slots, blocks, held_pad, part * groups, groups
        )
        sums = sums.reshape(n_bus, n_line // SUM_CHUNKS, held_pad, sums.shape[-1])
        pieces.append(halve_over_bus(sums, masks if part % 2 else masks[::-1], jnp.bfloat16))
    sums = jnp.concatenate(pieces, axis=0)
    sums = lax.psum_scatter(sums, "line", scatter_dimension=0, tiled=True)[0]
    return sums[:held]


def solution(mesh):
    placed = (
        P("line", "bus"),
        P("bus", "line"),
        P("line", None),
        P("line"),
        P("line"),
        P("line"),
        P("bus"),
    )
    return jax.shard_map(
        local, mesh=mesh, in_specs=placed, out_specs=P(("line", "bus"), None), check_vma=False
    )
```
